32 devices in a mesh: gx: 4 (over z), yz: 8 (over y, x, core).
Axes of the slice: x: 2, y: 2, z: 4, core: 2. Of those that a mesh axis runs over, the one named last changes fastest.
Arguments:
- positions: bfloat16 [3, 8192], P(None, ('gx', 'yz')), may hold values from 0 to 1
- species: int32 [8192], P(('gx', 'yz')), may hold values from 0 to 5
- features: bfloat16 [8192, 512], P(('gx', 'yz')), may hold values from -6 to 6
- move_dest: int32 [64], P(('gx', 'yz')), may hold values from 0 to 7, as said below
- move_slot: int32 [64], P(('gx', 'yz')), may hold values from 0 to 1, as said below
- halo_list: int32 [1024], P(('gx', 'yz')), may hold values from 0 to 255
- neighbours: int32 [8192, 64], P(('gx', 'yz')), may hold values from 0 to 383, as said below
- neighbour_count: int32 [8192], P(('gx', 'yz')), may hold values from 16 to 64
- wave_index: int32 [3, 4096], replicated, may hold values from -16 to 16, as said below
- radial_in: bfloat16 [8, 64], replicated, may hold values from -2 to 2
- radial_mid: bfloat16 [2, 64, 64], replicated, may hold values from -0.75 to 0.75
- radial_out: bfloat16 [64, 512], replicated, may hold values from -0.75 to 0.75
- up_weight: bfloat16 [2, 128, 128], replicated, may hold values from -0.5 to 0.5
- prod_weight: float32 [6, 640], replicated, may hold values from -4 to 4
- out_weight: bfloat16 [2, 128, 128], replicated, may hold values from -0.5 to 0.5
- skip_weight: bfloat16 [2, 128, 128], replicated, may hold values from -0.5 to 0.5
- charge_weight: bfloat16 [128, 8], replicated, may hold values from -0.5 to 0.5
- field_weight: float32 [8, 128], replicated, may hold values from -2 to 2
- read_weight: bfloat16 [128, 16], replicated, may hold values from -0.5 to 0.5
- read_vector: float32 [16], replicated, may hold values from -1.5 to 1.5
- force_weight: float32 [128], replicated, may hold values from -0.5 to 0.5
Outputs:
- forces: float32 [3, 8192], P(None, ('gx', 'yz'))
- energies: float32 [8192], P(('gx', 'yz'))
The draws below stay inside these ranges and needn't reach their ends.
Inputs may be any that keep to these rules, and one draw needn't show every extreme that they name: `move_dest`: the destination lies in the same gx row. Exactly 2 blocks of each device go to other devices, at most one to any one device, and each device receives exactly 2 blocks; the others stay. `move_slot`: the 2 blocks that a device holds after the move take its 2 slots once each. `neighbours`: row of the device's table: its working atoms, then the ghosts from gx - 1, gx + 1, yz - 1, yz + 1. Never the atom itself; slots from neighbour_count on are padding. `wave_index`: row 0 runs from 1 to 8, row 1 from -16 to 16, row 2 from -2 to 2.
All inputs are finite; a program needn't handle non-finite values.
Results may differ from the reference program's by a relative error of at most 0.0028.
Values may be sent and summed in bfloat16 or wider, within the bound.
A program may use at most 64 MiB of HBM per device.

```python
import math
import jax
import jax.numpy as jnp
from jax import lax

C = 128
Q = 8
K = 4096
NRAD = 8
RAD_H = 64
READ_H = 16
NSPEC = 6
MAXNB = 64
BLK = 128
MOVES = 2
A_DEV = 256
HALO = 32
NB_DEV = 2
DOM_X = 4
DOM_Y = 8
ATOMS = 8192
HALOS = 1024


def shuffled_offsets(subkey):
    return jax.random.permutation(subkey, DOM_Y - 1)[:MOVES].astype(jnp.int32) + 1


def shuffled_blocks(subkey):
    return jax.random.permutation(subkey, NB_DEV).astype(jnp.int32)


def plan_tables(key):
    plan_key = jax.random.fold_in(key, 4242)
    key_offsets, key_order, key_slots = jax.random.split(plan_key, 3)
    devices = DOM_X * DOM_Y
    offsets = jax.vmap(shuffled_offsets)(jax.random.split(key_offsets, DOM_X))
    block_order = jax.vmap(shuffled_blocks)(jax.random.split(key_order, devices))
    slot_order = jax.vmap(shuffled_blocks)(jax.random.split(key_slots, devices))
    device_ids = jnp.arange(devices, dtype=jnp.int32)
    row_of = device_ids // DOM_Y
    column_of = device_ids % DOM_Y
    rounds = jnp.arange(NB_DEV, dtype=jnp.int32)
    padded = jnp.concatenate([offsets, jnp.zeros((DOM_X, NB_DEV - MOVES), jnp.int32)], axis=1)
    dest_round = (column_of[:, None] + padded[row_of]) % DOM_Y
    dest_device = row_of[:, None] * DOM_Y + dest_round
    slot_round = slot_order[dest_device, jnp.broadcast_to(rounds[None, :], dest_device.shape)]
    inverse = jnp.argsort(block_order, axis=1).astype(jnp.int32)
    destination = jnp.take_along_axis(dest_round, inverse, axis=1)
    slot_table = jnp.take_along_axis(slot_round, inverse, axis=1)
    return (destination.reshape(-1).astype(jnp.int32), slot_table.reshape(-1).astype(jnp.int32))


def draw_move_dest(key, part):
    return plan_tables(key)[0]


def draw_move_slot(key, part):
    return plan_tables(key)[1]


def draw_neighbours(key, part):
    table_size = A_DEV + 4 * HALO
    drawn_rows = jax.random.randint(jax.random.fold_in(key, 31), (ATOMS, MAXNB), 0, table_size - 1, dtype=jnp.int32)
    own_row = (jnp.arange(ATOMS, dtype=jnp.int32) % A_DEV)[:, None]
    return drawn_rows + (drawn_rows >= own_row).astype(jnp.int32)


def draw_wave_index(key, part):
    subkeys = jax.random.split(jax.random.fold_in(key, 57), 3)
    along_x = jax.random.randint(subkeys[0], (K,), 1, 2 * DOM_X + 1, dtype=jnp.int32)
    along_y = jax.random.randint(subkeys[1], (K,), -2 * DOM_Y, 2 * DOM_Y + 1, dtype=jnp.int32)
    along_z = jax.random.randint(subkeys[2], (K,), -2, 3, dtype=jnp.int32)
    return jnp.stack([along_x, along_y, along_z])


def place_ends(result, key, low, top_value):
    longest = result.shape.index(max(result.shape))
    spots = []
    for shift in (0, 1):
        where = [jax.random.randint(jax.random.fold_in(key, axis), (), 0, length) for axis, length in enumerate(result.shape)]
        where[longest] = (where[longest] + shift) % result.shape[longest]
        spots.append(tuple(where))
    return result.at[spots[0]].set(low).at[spots[1]].set(top_value)


def steps_of(rng, dims, cuts, low, largest):
    level, own = 1.0, jax.random.fold_in(rng, 6)
    for dim, shards_of in cuts:
        steps = jnp.exp(jax.random.uniform(jax.random.fold_in(own, dim), (shards_of,), jnp.float32, low / len(cuts), largest / len(cuts)))
        level = level * jnp.repeat(steps, dims[dim] // shards_of).reshape([-1 if axis == dim else 1 for axis in range(len(dims))])
    return level


def gaussian(key, extent, spread, bound, cuts=(), held_as=jnp.bfloat16):
    gain = steps_of(key, extent, cuts, -0.22, 0.18) if cuts else 1.0
    values = jax.random.normal(key, extent, jnp.float32) * spread * gain
    return jnp.minimum(jnp.maximum(values, -bound), bound).astype(held_as)


def setup_inputs(seed: int = 0) -> dict:
    keys = jax.random.split(jax.random.key(seed), 22)
    positions = jnp.clip(1.0 * jax.random.uniform(keys[0], (3, ATOMS), jnp.float32) ** steps_of(keys[0], (3, ATOMS), ((1, 32),), -0.2, 0.2), 0.0, 1.0).astype(jnp.bfloat16)
    species = place_ends(jax.random.randint(keys[1], (ATOMS,), 0, NSPEC), jax.random.fold_in(keys[1], 1), 0, NSPEC - 1).astype(jnp.int32)
    features = gaussian(keys[2], (ATOMS, 4 * C), 1.0, 6.0, ((0, 32),))
    move_dest = draw_move_dest(jax.random.fold_in(keys[21], 71), 0)
    move_slot = draw_move_slot(jax.random.fold_in(keys[21], 71), 0)
    halo_list = place_ends(jax.random.randint(keys[5], (HALOS,), 0, A_DEV), jax.random.fold_in(keys[5], 1), 0, A_DEV - 1).astype(jnp.int32)
    neighbours = draw_neighbours(jax.random.fold_in(keys[21], 71), 0)
    neighbour_count = place_ends(jax.random.randint(keys[7], (ATOMS,), MAXNB // 4, MAXNB + 1), jax.random.fold_in(keys[7], 1), MAXNB // 4, MAXNB).astype(jnp.int32)
    wave_index = draw_wave_index(jax.random.fold_in(keys[21], 71), 0)
    radial_in = gaussian(keys[9], (NRAD, RAD_H), NRAD ** -0.5, 2.0)
    radial_mid = gaussian(keys[10], (2, RAD_H, RAD_H), RAD_H ** -0.5, 0.75)
    radial_out = gaussian(keys[11], (RAD_H, 4 * C), RAD_H ** -0.5, 0.75)
    up_weight = gaussian(keys[12], (2, C, C), C ** -0.5, 0.5)
    prod_weight = gaussian(keys[13], (NSPEC, 5 * C), 0.7, 4.0, (), jnp.float32)
    out_weight = gaussian(keys[14], (2, C, C), C ** -0.5, 0.5)
    skip_weight = gaussian(keys[15], (2, C, C), C ** -0.5, 0.5)
    charge_weight = gaussian(keys[16], (C, Q), C ** -0.5, 0.5)
    field_weight = gaussian(keys[17], (Q, C), Q ** -0.5, 2.0, (), jnp.float32)
    read_weight = gaussian(keys[18], (C, READ_H), C ** -0.5, 0.5)
    read_vector = gaussian(keys[19], (READ_H,), READ_H ** -0.5, 1.5, (), jnp.float32)
    force_weight = gaussian(keys[20], (C,), C ** -0.5, 0.5, (), jnp.float32)
    return dict(positions=positions, species=species, features=features, move_dest=move_dest, move_slot=move_slot, halo_list=halo_list, neighbours=neighbours, neighbour_count=neighbour_count, wave_index=wave_index, radial_in=radial_in, radial_mid=radial_mid, radial_out=radial_out, up_weight=up_weight, prod_weight=prod_weight, out_weight=out_weight, skip_weight=skip_weight, charge_weight=charge_weight, field_weight=field_weight, read_weight=read_weight, read_vector=read_vector, force_weight=force_weight)


highest = lax.Precision.HIGHEST
two_pi = 2.0 * math.pi
cutoff_radius = 3.5
basis_sharpness = 4.0
ewald_width = 0.1
ewald_scale = 0.01
atom_step = 64
wave_step = 512

def wave_vectors(wave_index, domains_x, domains_y):
    scales = jnp.array([two_pi / domains_x, two_pi / domains_y, two_pi], jnp.float32)
    wavevectors = wave_index.astype(jnp.float32) * scales[:, None]
    squared = lax.optimization_barrier(jnp.sum(wavevectors * wavevectors, axis=0))
    prefactor = 8.0 * math.pi * ewald_scale / (domains_x * domains_y)
    weights = prefactor * jnp.exp(-0.5 * ewald_width * ewald_width * squared) / squared
    return (wavevectors, weights)

def phase_of(absolute, wavevectors):
    return absolute[0][:, None] * wavevectors[0][None, :] + absolute[1][:, None] * wavevectors[1][None, :] + absolute[2][:, None] * wavevectors[2][None, :]

def structure_terms(absolute, charges, wavevectors):
    stride = math.gcd(wavevectors.shape[1], wave_step)
    block_count = wavevectors.shape[1] // stride

    def one_block(block_index):
        wave_block = lax.dynamic_slice_in_dim(wavevectors, block_index * stride, stride, 1)
        phases = phase_of(absolute, wave_block)
        real_part = jnp.einsum('ak,aq->kq', jnp.cos(phases), charges, precision=highest)
        imag_part = jnp.einsum('ak,aq->kq', jnp.sin(phases), charges, precision=highest)
        return (real_part, imag_part)
    real_part, imag_part = lax.map(one_block, jnp.arange(block_count, dtype=jnp.int32))
    latent = charges.shape[1]
    return (real_part.reshape(-1, latent), imag_part.reshape(-1, latent))

def field_terms(absolute, wavevectors, weights, total_real, total_imag):
    scaled_real = weights[:, None] * total_real
    scaled_imag = weights[:, None] * total_imag
    right_cos = jnp.concatenate([scaled_real] + [-wavevectors[direction][:, None] * scaled_imag for direction in range(3)], axis=1)
    right_sin = jnp.concatenate([scaled_imag] + [wavevectors[direction][:, None] * scaled_real for direction in range(3)], axis=1)
    stride = math.gcd(wavevectors.shape[1], wave_step)
    block_count = wavevectors.shape[1] // stride

    def accumulate(block_index, running):
        wave_block = lax.dynamic_slice_in_dim(wavevectors, block_index * stride, stride, 1)
        phases = phase_of(absolute, wave_block)
        cos_right = lax.dynamic_slice_in_dim(right_cos, block_index * stride, stride, 0)
        sin_right = lax.dynamic_slice_in_dim(right_sin, block_index * stride, stride, 0)
        running = running + jnp.dot(jnp.cos(phases), cos_right, precision=highest)
        return running + jnp.dot(jnp.sin(phases), sin_right, precision=highest)
    initial = jnp.zeros((absolute.shape[1], right_cos.shape[1]), jnp.float32)
    return lax.fori_loop(0, block_count, accumulate, initial)

def project_pair(feature, weights):
    channels = weights.shape[1]
    row_count = feature.shape[0]
    scalar = jnp.dot(feature[:, :channels], weights[0], preferred_element_type=jnp.float32)
    vector = jnp.dot(feature[:, channels:].reshape(row_count * 3, channels), weights[1], preferred_element_type=jnp.float32)
    return jnp.concatenate([scalar, vector.reshape(row_count, 3 * channels)], axis=1)

def edge_products(table_pos, table_up, centre_pos, nbr_rows, nbr_live, coeffs, radial_in, radial_mid, radial_out):
    atom_count, slot_count = nbr_rows.shape
    edge_count = atom_count * slot_count
    flat_rows = nbr_rows.reshape(edge_count)
    offset = (table_pos[:, flat_rows].reshape(3, atom_count, slot_count) - centre_pos[:, :, None]).reshape(3, edge_count)
    distance = jnp.sqrt(lax.optimization_barrier(jnp.sum(offset * offset, axis=0)))
    scaled_dist = distance / cutoff_radius
    envelope = 1.0 - 28.0 * scaled_dist ** 6 + 48.0 * scaled_dist ** 7 - 21.0 * scaled_dist ** 8
    alive_mask = (jnp.arange(slot_count, dtype=jnp.int32)[None, :] < nbr_live[:, None]).astype(jnp.float32).reshape(edge_count)
    basis_count = radial_in.shape[0]
    centres = jnp.arange(basis_count, dtype=jnp.float32) * (cutoff_radius / (basis_count - 1))
    radial_basis = jnp.exp(-basis_sharpness * (distance[:, None] - centres[None, :]) ** 2).astype(jnp.bfloat16)
    hidden = jax.nn.silu(jnp.dot(radial_basis, radial_in, preferred_element_type=jnp.float32)).astype(jnp.bfloat16)
    hidden = jax.nn.silu(jnp.dot(hidden, radial_mid[0], preferred_element_type=jnp.float32)).astype(jnp.bfloat16)
    hidden = jax.nn.silu(jnp.dot(hidden, radial_mid[1], preferred_element_type=jnp.float32)).astype(jnp.bfloat16)
    radial = (jnp.dot(hidden, radial_out, preferred_element_type=jnp.float32) * (envelope * alive_mask)[:, None]).astype(jnp.bfloat16)
    channels = radial.shape[1] // 4
    gathered = table_up[flat_rows]

    def column_block(source, number):
        return source[:, number * channels:(number + 1) * channels].astype(jnp.float32)
    norm_factor = 1.0 / math.sqrt(slot_count)

    def neighbour_sum(values):
        return lax.optimization_barrier(jnp.sum(values.reshape(atom_count, slot_count, channels), axis=1)) * norm_factor
    up_scalar = column_block(gathered, 0)
    up_vector = [column_block(gathered, 1 + direction) for direction in range(3)]
    along = up_vector[0] * offset[0][:, None] + up_vector[1] * offset[1][:, None] + up_vector[2] * offset[2][:, None]
    scalar_msg = neighbour_sum(column_block(radial, 0) * up_scalar + column_block(radial, 1) * along)
    radial_scalar = column_block(radial, 2) * up_scalar
    radial_vector = column_block(radial, 3)
    vector_msg = [neighbour_sum(radial_scalar * offset[direction][:, None] + radial_vector * up_vector[direction]) for direction in range(3)]
    square_sum = vector_msg[0] * vector_msg[0] + vector_msg[1] * vector_msg[1] + vector_msg[2] * vector_msg[2]
    path_weights = [coeffs[:, number * channels:(number + 1) * channels] for number in range(5)]
    scalar_prod = path_weights[0] * scalar_msg + path_weights[1] * scalar_msg * scalar_msg + path_weights[2] * square_sum
    vector_prod = [path_weights[3] * vector_msg[direction] + path_weights[4] * scalar_msg * vector_msg[direction] for direction in range(3)]
    return jnp.concatenate([scalar_prod] + vector_prod, axis=1).astype(jnp.bfloat16)

def atom_results(work_feat, products, charges, efield, out_weight, skip_weight, field_weight, read_weight, read_vector, force_weight):
    channels = out_weight.shape[1]
    latent = charges.shape[1]
    mixed_feat = project_pair(products, out_weight) + project_pair(work_feat, skip_weight)
    potential = efield[:, :latent]
    scalars = mixed_feat[:, :channels] + jnp.dot(potential, field_weight, precision=highest)
    readout = jax.nn.silu(jnp.dot(scalars.astype(jnp.bfloat16), read_weight, preferred_element_type=jnp.float32))
    energy = jnp.dot(readout, read_vector, precision=highest) + 0.5 * lax.optimization_barrier(jnp.sum(charges * potential, axis=1))
    forces = [jnp.dot(mixed_feat[:, (1 + direction) * channels:(2 + direction) * channels], force_weight, precision=highest) + lax.optimization_barrier(jnp.sum(charges * efield[:, (1 + direction) * latent:(2 + direction) * latent], axis=1)) for direction in range(3)]
    return jnp.stack(forces + [energy])

def take_columns(matrix, chosen):
    return matrix[:, chosen]

def take_rows(matrix, chosen):
    return matrix[chosen]

def reference(positions, species, features, move_dest, move_slot, halo_list, neighbours, neighbour_count, wave_index, radial_in, radial_mid, radial_out, up_weight, prod_weight, out_weight, skip_weight, charge_weight, field_weight, read_weight, read_vector, force_weight):
    devices = DOM_X * DOM_Y
    blocks = NB_DEV
    channels = C
    home_device = jnp.arange(devices * blocks, dtype=jnp.int32) // blocks
    target = ((home_device // DOM_Y * DOM_Y + move_dest) * blocks + move_slot).astype(jnp.int32)
    pos_blocks = positions.astype(jnp.float32).reshape(3, devices * blocks, BLK)
    work_pos = jnp.zeros_like(pos_blocks).at[:, target].set(pos_blocks).reshape(3, devices, A_DEV).transpose(1, 0, 2)
    spec_blocks = species.reshape(devices * blocks, BLK)
    work_species = jnp.zeros_like(spec_blocks).at[target].set(spec_blocks).reshape(devices, A_DEV)
    feat_blocks = features.reshape(devices * blocks, BLK, 4 * channels)
    work_feat = jnp.zeros_like(feat_blocks).at[target].set(feat_blocks).reshape(devices, A_DEV, 4 * channels)
    send_lists = halo_list.reshape(devices, HALO)
    send_pos = jax.vmap(take_columns)(work_pos, send_lists).reshape(DOM_X, DOM_Y, 3, HALO)
    send_feat = jax.vmap(take_rows)(work_feat, send_lists).reshape(DOM_X, DOM_Y, HALO, 4 * channels)
    unit_axes = jnp.eye(3, dtype=jnp.float32)
    ghost_pos = [jnp.roll(send_pos, 1, axis=0) - unit_axes[0][:, None], jnp.roll(send_pos, -1, axis=0) + unit_axes[0][:, None], jnp.roll(send_pos, 1, axis=1) - unit_axes[1][:, None], jnp.roll(send_pos, -1, axis=1) + unit_axes[1][:, None]]
    ghost_feat = [jnp.roll(send_feat, 1, axis=0), jnp.roll(send_feat, -1, axis=0), jnp.roll(send_feat, 1, axis=1), jnp.roll(send_feat, -1, axis=1)]
    table_pos = jnp.concatenate([work_pos] + [ghost.reshape(devices, 3, HALO) for ghost in ghost_pos], axis=2)
    table_feat = jnp.concatenate([work_feat] + [ghost.reshape(devices, HALO, 4 * channels) for ghost in ghost_feat], axis=1)
    device_ids = jnp.arange(devices, dtype=jnp.int32)
    anchor = jnp.stack([(device_ids // DOM_Y).astype(jnp.float32), (device_ids % DOM_Y).astype(jnp.float32), jnp.zeros((devices,), jnp.float32)], axis=1)
    absolute = work_pos + anchor[:, :, None]
    charges = jnp.dot(work_feat[:, :, :channels].reshape(devices * A_DEV, channels), charge_weight, preferred_element_type=jnp.float32).reshape(devices, A_DEV, Q)
    wavevectors, weights = wave_vectors(wave_index, DOM_X, DOM_Y)

    def add_device(running, inputs):
        part_real, part_imag = structure_terms(inputs[0], inputs[1], wavevectors)
        return ((running[0] + part_real, running[1] + part_imag), None)
    initial = (jnp.zeros((K, Q), jnp.float32), jnp.zeros((K, Q), jnp.float32))
    (total_real, total_imag), ignored = lax.scan(add_device, initial, (absolute, charges))

    def one_device(inputs):
        tab_pos, tab_feat, own_pos, own_abs, own_species, own_feat, nbr_rows, nbr_live, own_charges = inputs
        table_up = project_pair(tab_feat, up_weight).astype(jnp.bfloat16)
        onehot = (own_species[:, None] == jnp.arange(NSPEC, dtype=jnp.int32)[None, :]).astype(jnp.float32)
        coeffs = jnp.dot(onehot, prod_weight, precision=highest)
        block_count = A_DEV // atom_step

        def edge_block(pieces):
            return edge_products(tab_pos, table_up, pieces[2], pieces[0], pieces[1], pieces[3], radial_in, radial_mid, radial_out)
        products = lax.map(edge_block, (nbr_rows.reshape(block_count, atom_step, MAXNB), nbr_live.reshape(block_count, atom_step), own_pos.reshape(3, block_count, atom_step).transpose(1, 0, 2), coeffs.reshape(block_count, atom_step, 5 * channels))).reshape(A_DEV, 4 * channels)
        efield = field_terms(own_abs, wavevectors, weights, total_real, total_imag)
        return atom_results(own_feat, products, own_charges, efield, out_weight, skip_weight, field_weight, read_weight, read_vector, force_weight)
    results = lax.map(one_device, (table_pos, table_feat, work_pos, absolute, work_species, work_feat, neighbours.reshape(devices, A_DEV, MAXNB), neighbour_count.reshape(devices, A_DEV), charges))
    res_blocks = results.reshape(devices, 4, blocks, BLK).transpose(1, 0, 2, 3).reshape(4, devices * blocks, BLK)
    home_res = res_blocks[:, target].reshape(4, devices * A_DEV)
    return (home_res[:3], home_res[3])
```

```python
import functools
import math

import jax
import jax.numpy as jnp
from jax import lax
from jax.experimental import pallas as pl
from jax.experimental.pallas import tpu as pltpu
from jax.sharding import PartitionSpec as P

highest = lax.Precision.HIGHEST
two_pi = 2.0 * math.pi
cutoff_radius = 3.5
basis_sharpness = 4.0
ewald_width = 0.1
ewald_scale = 0.01
z_reach = 2
lanes = 128
f32 = jnp.float32
bf16 = jnp.bfloat16

VMEM = pl.BlockSpec(memory_space=pltpu.VMEM)
SMEM = pl.BlockSpec(memory_space=pltpu.SMEM)
NT = (((1,), (1,)), ((), ()))
TN = (((0,), (0,)), ((), ()))


def nt(a, b, precision=None):
    return lax.dot_general(a, b, NT, precision=precision, preferred_element_type=f32)


def tn(a, b, precision=None):
    return lax.dot_general(a, b, TN, precision=precision, preferred_element_type=f32)


def mm(a, b, precision=None):
    return jnp.dot(a, b, precision=precision, preferred_element_type=f32)


def iota(shape, dim):
    return lax.broadcasted_iota(jnp.int32, shape, dim)


def silu(v):
    half = 0.5 * v
    return half + half * jnp.tanh(half)


def turn_cos_sin(turns):
    frac = turns - jnp.floor(turns + 0.5)
    angle = two_pi * frac
    return jnp.cos(angle), jnp.sin(angle)


def send_kernel(dest, slot, feat, pos, species, out):
    peers, block, _ = out.shape
    atoms, width = feat.shape
    blocks = atoms // block
    rows = jnp.concatenate(
        [pos[...].astype(f32), species[...].astype(f32), jnp.zeros((lanes - 4, atoms), f32)], axis=0
    )
    cols = rows.T
    lane = iota((block, lanes), 1)
    for d in range(peers):
        total = jnp.zeros((block, width), f32)
        side = jnp.zeros((block, lanes), f32)
        for b in range(blocks):
            chosen = jnp.where(dest[b] == d, 1.0, 0.0).astype(f32)
            total = total + chosen * feat[b * block : (b + 1) * block, :].astype(f32)
            mark = (slot[b] + 1).astype(f32)
            part = jnp.where(lane == 4, mark, cols[b * block : (b + 1) * block, :])
            side = side + chosen * part
        out[d, :, :width] = total.astype(bf16)
        out[d, :, width:] = side.astype(bf16)


def arrive_kernel(recv, halo, work, send, codes):
    peers, block, full = recv.shape
    atoms = work.shape[0]
    blocks = atoms // block
    width = full - lanes
    for s in range(blocks):
        total = jnp.zeros((block, full), f32)
        for d in range(peers):
            mark = recv[d, :, width + 4 : width + 5].astype(f32)
            total = total + jnp.where(mark == s + 1.0, 1.0, 0.0) * recv[d].astype(f32)
        work[s * block : (s + 1) * block, :] = total.astype(bf16)
    for d in range(peers):
        codes[d : d + 1, :] = jnp.broadcast_to(
            recv[d, 0:1, width + 4 : width + 5].astype(f32), (1, lanes)
        )
    count = halo.shape[0]
    pick = (halo[...] == iota((count, atoms), 1)).astype(f32).astype(bf16)
    send[...] = mm(pick, work[...]).astype(bf16)


def xz_factors(x_turns, z_turns, nx):
    steps = (iota((nx, x_turns.shape[1]), 0) + 1).astype(f32)
    xc, xs = turn_cos_sin(steps * x_turns)
    cos_rows, sin_rows = [], []
    for m in range(-z_reach, z_reach + 1):
        zc, zs = turn_cos_sin(m * z_turns)
        cos_rows.append(xc * zc - xs * zs)
        sin_rows.append(xc * zs + xs * zc)
    return jnp.concatenate(cos_rows, axis=0), jnp.concatenate(sin_rows, axis=0)


def wave_kernel(gx, yz, nyp, place, work, charge_t, partial, phases, charges):
    atoms, full = work.shape
    channels = charge_t.shape[1]
    pos = work[:, full - lanes :].astype(f32).T
    x_turns = (pos[0:1] + place[0]) * (1.0 / gx)
    y_turns = (pos[1:2] + place[1]) * (1.0 / yz)
    nx = 2 * gx
    xzc, xzs = xz_factors(x_turns, pos[2:3], nx)
    yc, ys = turn_cos_sin(iota((nyp, atoms), 0).astype(f32) * y_turns)
    q = nt(charge_t[...], work[:, :channels])
    pairs, latent = xzc.shape[0], q.shape[0]
    real = (xzc[:, None, :] * q[None]).reshape(pairs * latent, atoms)
    imag = (xzs[:, None, :] * q[None]).reshape(pairs * latent, atoms)
    ycs = jnp.concatenate([yc, ys], axis=0)
    partial[: 2 * nyp, :] = nt(ycs, real, highest)
    partial[2 * nyp :, :] = nt(ycs, imag, highest)
    phases[: 2 * nyp, :] = ycs
    phases[2 * nyp : 2 * nyp + pairs, :] = xzc
    phases[2 * nyp + pairs :, :] = xzs
    charges[...] = q


def grid_kernel(gx, yz, nyp, latent, wave, out):
    nx = 2 * gx
    cols = out.shape[1]
    count = wave.shape[1]
    group = iota((cols, count), 0) // latent
    code = (wave[2:3, :] + z_reach) * nx + wave[0:1, :] - 1
    hot = (group == code).astype(f32).astype(bf16)
    row = iota((nyp, count), 0)
    plus = (row == wave[1:2, :]).astype(f32).astype(bf16)
    minus = ((row == -wave[1:2, :]) & (row > 0)).astype(f32).astype(bf16)
    times = nt(jnp.concatenate([plus, minus], axis=0), hot)
    ny = (iota((2 * nyp, cols), 0) % nyp).astype(f32)
    pair = iota((2 * nyp, cols), 1) // latent
    wx = ((pair % nx) + 1).astype(f32) * (two_pi / gx)
    wz = ((pair // nx) - z_reach).astype(f32) * two_pi
    wy = ny * (two_pi / yz)
    squared = wx * wx + wy * wy + wz * wz
    prefactor = 8.0 * math.pi * ewald_scale / (gx * yz)
    out[...] = times * (prefactor * jnp.exp(-0.5 * ewald_width * ewald_width * squared) / squared)


def table_kernel(work, g0, g1, g2, g3, up, table_up, table_pos):
    full = work.shape[1]
    width = full - lanes
    channels = up.shape[1]
    feat = jnp.concatenate([r[...] for r in (work, g0, g1, g2, g3)], axis=0)
    for part in range(4):
        table_up[:, part * channels : (part + 1) * channels] = mm(
            feat[:, part * channels : (part + 1) * channels], up[min(part, 1)]
        ).astype(bf16)
    lane = iota((1, lanes), 1)
    sides = [work[:, width:].astype(f32)]
    for ref, axis, shift in ((g0, 0, -1.0), (g1, 0, 1.0), (g2, 1, -1.0), (g3, 1, 1.0)):
        sides.append(ref[:, width:].astype(f32) + jnp.where(lane == axis, shift, 0.0))
    pos = jnp.concatenate(sides, axis=0).T[:8]
    high = pos.astype(bf16)
    low = (pos - high.astype(f32)).astype(bf16)
    table_pos[...] = jnp.concatenate([high.astype(f32), low.astype(f32)], axis=0).astype(bf16)


def edge_kernel(
    slots, table_up, table_pos, nbr, centre, side, prod, rin_t, mid_t, rout, products
):
    table = table_up.shape[0]
    atoms = side.shape[0]
    channels = products.shape[1] // 4
    edges = atoms * slots
    row = nbr[0]
    hot_t = (iota((table, edges), 0) == row).astype(f32).astype(bf16)
    spread = (iota((atoms, edges), 0) == iota((atoms, edges), 1) // slots).astype(f32).astype(bf16)
    both = mm(table_pos[...], hot_t)
    own = mm(centre[0], spread)
    r = both[:8] + both[8:] - own[:8]
    dist = jnp.sqrt(r[0:1] * r[0:1] + r[1:2] * r[1:2] + r[2:3] * r[2:3])
    u = dist * (1.0 / cutoff_radius)
    u2 = u * u
    u6 = u2 * u2 * u2
    env = 1.0 + u6 * (-28.0 + u * (48.0 - 21.0 * u))
    live = (iota((1, edges), 1) % slots).astype(f32) < own[4:5]
    env = jnp.where(live, env, 0.0)
    nrad = 8
    centres = iota((2 * nrad, edges), 0).astype(f32) * (cutoff_radius / (nrad - 1))
    off = dist - centres
    basis = jnp.exp(-basis_sharpness * off * off).astype(bf16)
    h = silu(mm(rin_t[...], basis)).astype(bf16)
    h = silu(mm(mid_t[0], h)).astype(bf16)
    h = silu(mm(mid_t[1], h)) * env
    cols = jnp.concatenate(
        [h, r[:3], row.astype(f32), jnp.zeros((lanes - h.shape[0] - 4, edges), f32)], axis=0
    ).T
    base = h.shape[0]
    hot = (iota((edges, table), 1).astype(f32) == cols[:, base + 3 : base + 4]).astype(f32)
    up = mm(hot.astype(bf16), table_up[...])
    radial = mm(cols[:, :base].astype(bf16), rout[...])

    def part(source, k):
        return source[:, k * channels : (k + 1) * channels]

    rm = [cols[:, base + m : base + m + 1] for m in range(3)]
    u1 = [part(up, 1 + m) for m in range(3)]
    along = rm[0] * u1[0] + rm[1] * u1[1] + rm[2] * u1[2]

    def total(v):
        return jnp.sum(v.reshape(atoms, slots, channels), axis=1) * (1.0 / math.sqrt(slots))

    a0 = total(part(radial, 0) * part(up, 0) + part(radial, 1) * along)
    ru = part(radial, 2) * part(up, 0)
    rd = part(radial, 3)
    a1 = [total(ru * rm[m] + rd * u1[m]) for m in range(3)]
    kind = side[:, 3:4].astype(f32)
    p = jnp.zeros((atoms, prod.shape[1]), f32)
    for s in range(prod.shape[0]):
        p = p + jnp.where(kind == float(s), prod[s : s + 1, :], 0.0)
    square = a1[0] * a1[0] + a1[1] * a1[1] + a1[2] * a1[2]
    b0 = part(p, 0) * a0 + part(p, 1) * a0 * a0 + part(p, 2) * square
    products[:, :channels] = b0.astype(bf16)
    for m in range(3):
        products[:, (1 + m) * channels : (2 + m) * channels] = (
            part(p, 3) * a1[m] + part(p, 4) * a0 * a1[m]
        ).astype(bf16)


def final_kernel(
    gx, yz, nyp, sums, grid, phases, charges, products, work, ow, sw, fieldw, read_t, rvec, fw,
    codes, out,
):
    channels = ow.shape[1]
    atoms = work.shape[0]
    total = sums[0]
    for d in range(1, sums.shape[0]):
        total = total + sums[d]
    cre, sre, cim, sim = [total[k * nyp : (k + 1) * nyp] for k in range(4)]
    gp, gm = grid[:nyp], grid[nyp:]
    pre, pim = gp * (cre - sim), gp * (cim + sre)
    mre, mim = gm * (cre + sim), gm * (cim - sre)
    sum_re, sum_im, dif_re, dif_im = pre + mre, pim + mim, pre - mre, pim - mim
    wy = iota(sum_re.shape, 0).astype(f32) * (two_pi / yz)
    ycs = phases[: 2 * nyp, :]
    q = charges[...]
    latent = q.shape[0]
    pairs = sum_re.shape[1] // latent

    def contract(first, second):
        left = jnp.concatenate([first, second], axis=0)
        return tn(left, ycs, highest).reshape(pairs, latent, atoms)

    v_re = contract(sum_re, dif_im)
    v_im = contract(sum_im, -dif_re)
    y_re = contract(wy * dif_re, wy * sum_im)
    y_im = contract(wy * dif_im, -wy * sum_re)
    xzc = phases[2 * nyp : 2 * nyp + pairs, :][:, None, :]
    xzs = phases[2 * nyp + pairs :, :][:, None, :]
    d_re = xzc * v_re + xzs * v_im
    d_im = xzc * v_im - xzs * v_re
    d_y = xzc * y_im - xzs * y_re
    nx = 2 * gx
    pair = iota((pairs, latent, atoms), 0)
    wx = ((pair % nx) + 1).astype(f32) * (two_pi / gx)
    wz = ((pair // nx) - z_reach).astype(f32) * two_pi
    potential = jnp.sum(d_re, axis=0)
    efield = [-jnp.sum(wx * d_im, axis=0), -jnp.sum(d_y, axis=0), -jnp.sum(wz * d_im, axis=0)]
    scal = (
        mm(products[:, :channels], ow[0])
        + mm(work[:, :channels], sw[0])
        + tn(potential, fieldw[...], highest)
    )
    readout = silu(nt(read_t[...], scal.astype(bf16)))
    energy = jnp.sum(readout * rvec[...], axis=0, keepdims=True) + 0.5 * jnp.sum(
        q * potential, axis=0, keepdims=True
    )
    rows = []
    for m in range(3):
        cut = slice((1 + m) * channels, (2 + m) * channels)
        vec = mm(products[:, cut], ow[1]) + mm(work[:, cut], sw[1])
        rows.append(
            nt(fw[...], vec, highest)[0:1] + jnp.sum(q * efield[m], axis=0, keepdims=True)
        )
    rows.append(energy)
    result = jnp.concatenate(rows + [jnp.zeros((4, atoms), f32)], axis=0)
    peers, _, block = out.shape
    for d in range(peers):
        mark = codes[d : d + 1, :block]
        acc = jnp.zeros((8, block), f32)
        for s in range(atoms // block):
            acc = acc + jnp.where(mark == s + 1.0, result[:, s * block : (s + 1) * block], 0.0)
        out[d] = acc


def home_kernel(dest, came, forces, energies):
    block = came.shape[2]
    for b in range(forces.shape[1] // block):
        got = came[dest[b]]
        forces[:, b * block : (b + 1) * block] = got[:3]
        energies[:, b * block : (b + 1) * block] = got[3:4]


def call(body, specs, out_shape, *args, **kwargs):
    many = isinstance(out_shape, (list, tuple))
    return pl.pallas_call(
        body,
        out_shape=out_shape,
        in_specs=specs,
        out_specs=[VMEM] * len(out_shape) if many else VMEM,
        **kwargs,
    )(*args)


def shape(dims, dtype):
    return jax.ShapeDtypeStruct(tuple(dims), dtype)


def on_device(
    positions,
    species,
    features,
    move_dest,
    move_slot,
    halo_list,
    neighbours,
    neighbour_count,
    wave_index,
    radial_in,
    radial_mid,
    radial_out,
    up_weight,
    prod_weight,
    out_weight,
    skip_weight,
    charge_weight,
    field_weight,
    read_weight,
    read_vector,
    force_weight,
):
    gx, yz = lax.axis_size("gx"), lax.axis_size("yz")
    atoms, width = features.shape
    blocks = move_dest.shape[0]
    block = atoms // blocks
    slots = neighbours.shape[1]
    full = width + lanes
    latent = charge_weight.shape[1]
    nyp = -(-(2 * yz + 1) // 8) * 8
    nx = 2 * gx
    pairs = nx * (2 * z_reach + 1)
    cols = pairs * latent
    halo = halo_list.shape[0]

    outgoing = call(
        send_kernel,
        [SMEM, SMEM, VMEM, VMEM, VMEM],
        shape((yz, block, full), bf16),
        move_dest,
        move_slot,
        features,
        positions,
        species.reshape(1, atoms),
    )
    recv = lax.all_to_all(outgoing, "yz", split_axis=0, concat_axis=0, tiled=True)
    work, send, codes = call(
        arrive_kernel,
        [VMEM, VMEM],
        [shape((atoms, full), bf16), shape((halo, full), bf16), shape((yz, lanes), f32)],
        recv,
        halo_list.reshape(halo, 1),
    )

    def ring(axis, step):
        count = lax.axis_size(axis)
        return lax.ppermute(send, axis, [(i, (i + step) % count) for i in range(count)])

    ghosts = [ring("gx", 1), ring("gx", -1), ring("yz", 1), ring("yz", -1)]
    grid = call(
        functools.partial(grid_kernel, gx, yz, nyp, latent),
        [VMEM],
        shape((2 * nyp, cols), f32),
        wave_index,
    )
    place = jnp.stack([lax.axis_index("gx"), lax.axis_index("yz")]).astype(f32)
    partial, phases, charges = call(
        functools.partial(wave_kernel, gx, yz, nyp),
        [SMEM, VMEM, VMEM],
        [
            shape((4 * nyp, cols), f32),
            shape((2 * nyp + 2 * pairs, atoms), f32),
            shape((latent, atoms), f32),
        ],
        place,
        work,
        charge_weight.T,
    )
    row_sums = jnp.sum(lax.all_gather(partial, "gx"), axis=0)
    sums = lax.all_gather(row_sums, "yz")
    table = atoms + 4 * halo
    table_up, table_pos = call(
        table_kernel,
        [VMEM] * 6,
        [shape((table, width), bf16), shape((16, table), bf16)],
        work,
        *ghosts,
        up_weight,
    )
    step = math.gcd(atoms, 32)
    steps = atoms // step
    edges = step * slots
    side = work[:, width:]
    own = jnp.concatenate([side[:, :4].T, neighbour_count.astype(bf16)[None]], axis=0)
    own = jnp.pad(own, ((0, 11), (0, 0))).reshape(16, steps, step).transpose(1, 0, 2)
    hidden = radial_mid.shape[1]
    nrad = radial_in.shape[0]
    rin_t = jnp.pad(radial_in.T, ((0, 0), (0, 16 - nrad)))

    def whole(a):
        return pl.BlockSpec(a.shape, lambda i: (0,) * a.ndim)

    mid_t = radial_mid.transpose(0, 2, 1)
    products = pl.pallas_call(
        functools.partial(edge_kernel, slots),
        out_shape=shape((atoms, width), bf16),
        grid=(steps,),
        in_specs=[
            whole(table_up),
            whole(table_pos),
            pl.BlockSpec((1, 1, edges), lambda i: (i, 0, 0)),
            pl.BlockSpec((1, 16, step), lambda i: (i, 0, 0)),
            pl.BlockSpec((step, lanes), lambda i: (i, 0)),
            whole(prod_weight),
            whole(rin_t),
            whole(mid_t),
            whole(radial_out),
        ],
        out_specs=pl.BlockSpec((step, width), lambda i: (i, 0)),
        compiler_params=pltpu.CompilerParams(vmem_limit_bytes=56 * 1024 * 1024),
    )(
        table_up,
        table_pos,
        neighbours.reshape(steps, 1, edges),
        own,
        side,
        prod_weight,
        rin_t,
        mid_t,
        radial_out,
    )
    back = call(
        functools.partial(final_kernel, gx, yz, nyp),
        [VMEM] * 13,
        shape((yz, 8, block), f32),
        sums,
        grid,
        phases,
        charges,
        products,
        work,
        out_weight,
        skip_weight,
        field_weight,
        read_weight.T,
        read_vector.reshape(-1, 1),
        jnp.broadcast_to(force_weight[None], (8, force_weight.shape[0])),
        codes,
    )
    came = lax.all_to_all(back, "yz", split_axis=0, concat_axis=0, tiled=True)
    forces, energies = call(
        home_kernel,
        [SMEM, VMEM],
        [shape((3, atoms), f32), shape((1, atoms), f32)],
        move_dest,
        came,
    )
    return (forces, energies.reshape(atoms))


def solution(mesh):
    split = P(("gx", "yz"))
    rows = P(("gx", "yz"), None)
    in_specs = (P(None, ("gx", "yz")), split, rows, split, split, split, rows, split) + (P(),) * 13
    out_specs = (P(None, ("gx", "yz")), split)
    return jax.shard_map(
        on_device, mesh=mesh, in_specs=in_specs, out_specs=out_specs, check_vma=False
    )
```
